32 devices in a mesh: groups: 2 (over x), seq: 16 (over z, y, core).
Axes of the slice: x: 2, y: 2, z: 4, core: 2. Of those that a mesh axis runs over, the one named last changes fastest.
Arguments:
- cache_keys: bfloat16 [131072, 1024], P(('groups', 'seq')), parts along dimension 0, may hold values from -48 to 48
- cache_values: bfloat16 [131072, 1024], P(('groups', 'seq')), parts along dimension 0, may hold values from -6 to 6
- sketch_matrix: float32 [1024, 160], replicated, may hold values from -6 to 6
- queries: bfloat16 [6, 8192], P('groups'), parts along dimension 0, may hold values from -2000 to 2000
- fresh_keys: bfloat16 [6, 1024], P('groups'), parts along dimension 0, may hold values from -20 to 20
- fresh_values: bfloat16 [6, 1024], P('groups'), parts along dimension 0, may hold values from -6 to 6
- chosen: int32 [6, 8, 256], P('groups'), parts along dimension 0, may hold values from 0 to 8191, as said below
- shard_counts: int32 [6, 8, 16], P('groups'), parts along dimension 0, may hold values from 0 to 48, as said below
- outliers: int32 [64], P('groups'), parts along dimension 0, may hold values from 0 to 8191, as said below
Outputs:
- attended: bfloat16 [6, 8192], P('groups', 'seq'), parts along dimension 0
- key_factor: float32 [131072, 160], P(('groups', 'seq')), parts along dimension 0
The draws below stay inside these ranges and needn't reach their ends.
There are 2 independent parts, one for each index of `groups`. The reference program is written for one: setup_inputs(seed, part) draws one part's arguments, and reference() takes and returns one part's arrays. A program takes and returns all parts, laid end to end along the dimension named above; an argument that names none is the same for every part. Nothing has to cross between parts.
Inputs may be any that keep to these rules, and one draw needn't show every extreme that they name: Each list chosen[t, g] holds distinct span numbers in ascending order, none of them an outlier span; shard s holds spans s * 512 to (s+1) * 512 - 1. shard_counts[t, g, s] is the number of entries of chosen[t, g] on shard s; they sum to 256; the most is 48, reached in every list. `outliers`: distinct span numbers in ascending order; at most 4 on one shard, reached on some shard.
All inputs are finite; a program needn't handle non-finite values.
Results may differ from the reference program's by a relative error of at most 0.0228.
Values may be sent and summed in bfloat16 or wider, within the bound.
A program may use at most 128 MiB of HBM per device.

```python
import jax
import jax.numpy as jnp
from jax import lax

KVH = 8
HD = 128
QH = 64
RANK = 160
SPAN = 8
STEPS = 3
SEL = 256
OUTL = 32
OMOST = 4
LEN_DEV = 4096
D_KV = 1024
GROUP = 8
LENGTH = 65536
CH_DEV = 512
TOTAL_CH = 8192
MOST = 48
N_SEQ = 16


def capped_deal(deal_key, total_items, cap_items, weights_row):
    hot_key, loop_key = jax.random.split(deal_key)
    hottest = jax.random.randint(hot_key, (), 0, N_SEQ)
    tally = jnp.zeros((N_SEQ,), jnp.int32).at[hottest].set(cap_items)

    def place_one(item_turn, tally_now):
        open_weight = jnp.where(tally_now >= cap_items, 0, weights_row)
        running = jnp.cumsum(open_weight)
        ticket = jax.random.randint(jax.random.fold_in(loop_key, item_turn), (), 0, running[-1])
        target_shard = jnp.sum((running <= ticket).astype(jnp.int32))
        return tally_now.at[target_shard].add(1)
    return lax.fori_loop(0, total_items - cap_items, place_one, tally)


def shard_ranks(rank_key, pushed):
    span_ids = jnp.arange(TOTAL_CH, dtype=jnp.int32)
    shard_of = span_ids // CH_DEV
    shuffled = jax.random.permutation(rank_key, TOTAL_CH).astype(jnp.int32)
    order_pos = jnp.zeros((TOTAL_CH,), jnp.int32).at[shuffled].set(span_ids)
    sort_key = shard_of * (2 * TOTAL_CH) + pushed * TOTAL_CH + order_pos
    ordering = jnp.argsort(sort_key)
    placed = jnp.zeros((TOTAL_CH,), jnp.int32).at[ordering].set(span_ids)
    return placed - shard_of * CH_DEV


def selection_tables(key):
    base_key = jax.random.fold_in(key, 7177)
    out_key, sel_key = jax.random.split(base_key)
    out_deal, out_rank = jax.random.split(out_key)
    outlier_counts = capped_deal(out_deal, OUTL, OMOST, jnp.ones((N_SEQ,), jnp.int32))
    span_ids = jnp.arange(TOTAL_CH, dtype=jnp.int32)
    shard_of = span_ids // CH_DEV
    outlier_rank = shard_ranks(out_rank, jnp.zeros((TOTAL_CH,), jnp.int32))
    is_outlier = outlier_rank < outlier_counts[shard_of]
    outlier_list = jnp.sort(jnp.where(is_outlier, span_ids, TOTAL_CH + span_ids))[:OUTL]

    def one_list(list_key):
        weight_key, deal_key, order_key = jax.random.split(list_key, 3)
        raw_weight = jax.random.randint(weight_key, (N_SEQ,), 1, 9)
        tally = capped_deal(deal_key, SEL, MOST, raw_weight * raw_weight)
        ranks = shard_ranks(order_key, is_outlier.astype(jnp.int32))
        taken = (ranks < tally[shard_of]) & jnp.logical_not(is_outlier)
        return (jnp.sort(jnp.where(taken, span_ids, TOTAL_CH + span_ids))[:SEL], tally)
    lists, tallies = jax.vmap(one_list)(jax.random.split(sel_key, STEPS * KVH))
    return (lists.reshape(STEPS, KVH, SEL), tallies.reshape(STEPS, KVH, N_SEQ), outlier_list)


def query_tables(key):
    base_key = jax.random.fold_in(key, 3131)
    key_query, key_fresh = jax.random.split(base_key, 2)
    query_rows = jnp.clip(jax.random.normal(key_query, (STEPS, QH, HD), jnp.float32), -5.0, 5.0)
    fresh_rows = jnp.clip(jax.random.normal(key_fresh, (STEPS, KVH, HD), jnp.float32), -5.0, 5.0)
    group_sum = jnp.sum(query_rows.reshape(STEPS, KVH, QH // KVH, HD), axis=2) / jnp.sqrt(jnp.float32(QH // KVH))
    strength = 5.0 * jnp.sqrt(jnp.float32(QH // KVH) / jnp.float32(HD))
    fresh_rows = jnp.clip(strength * group_sum + 0.3 * fresh_rows, -20.0, 20.0)
    return (query_rows.reshape(STEPS, QH * HD), fresh_rows.reshape(STEPS, KVH * HD))


def draw_cache_keys(key, part):
    raw_keys = jnp.clip(jax.random.normal(jax.random.fold_in(key, 5151), (LENGTH, D_KV), jnp.float32), -6.0, 6.0)
    levels = jnp.exp(jax.random.uniform(jax.random.fold_in(key, 5252), (D_KV,), jnp.float32, minval=jnp.log(0.5), maxval=jnp.log(2.0)))
    shard_of = jnp.arange(LENGTH, dtype=jnp.int32) // LEN_DEV
    block_of = jnp.arange(D_KV, dtype=jnp.int32) // (D_KV // N_SEQ)
    offset = (block_of[None, :] - shard_of[:, None]) % N_SEQ
    paired = (offset == 0) | (offset == 1) | (offset == N_SEQ // 2) | (offset == N_SEQ // 2 + 1)
    return (raw_keys * jnp.where(paired, 4.0, 1.0) * levels[None, :]).astype(jnp.bfloat16)


def draw_chosen(key, part):
    return selection_tables(key)[0]


def draw_shard_counts(key, part):
    return selection_tables(key)[1]


def draw_outliers(key, part):
    return selection_tables(key)[2]


def draw_queries(key, part):
    return query_tables(key)[0].astype(jnp.bfloat16)


def draw_fresh_keys(key, part):
    return query_tables(key)[1].astype(jnp.bfloat16)


def steps_of(rng, dims, cuts, least, largest):
    factor_of, own = 1.0, jax.random.fold_in(rng, 6)
    for dim, parts in cuts:
        draws = jnp.exp(jax.random.uniform(jax.random.fold_in(own, dim), (parts,), jnp.float32, least / len(cuts), largest / len(cuts)))
        factor_of = factor_of * jnp.repeat(draws, dims[dim] // parts).reshape([-1 if axis == dim else 1 for axis in range(len(dims))])
    return factor_of


def noise(stream_key, dims, scale, bound, shards=(), kind=jnp.bfloat16):
    result = jax.random.normal(stream_key, dims, jnp.float32) * scale
    if len(shards) > 0:
        result = steps_of(stream_key, dims, shards, -0.22, 0.18) * result
    return jnp.clip(result, min=-bound, max=bound).astype(kind)


def setup_inputs(seed: int = 0, part: int = 0) -> dict:
    streams_of = jax.random.split(jax.random.key(seed), 10)
    own_keys = jax.random.split(jax.random.fold_in(streams_of[9], part), 10)
    cache_keys = draw_cache_keys(jax.random.fold_in(jax.random.fold_in(streams_of[9], part), 71), part)
    cache_values = noise(own_keys[1], (LENGTH, D_KV), 1.0, 6.0, ((0, 16),))
    sketch_matrix = noise(streams_of[2], (D_KV, RANK), 1.0, 6.0, (), jnp.float32)
    queries = draw_queries(jax.random.fold_in(jax.random.fold_in(streams_of[9], part), 71), part)
    fresh_keys = draw_fresh_keys(jax.random.fold_in(jax.random.fold_in(streams_of[9], part), 71), part)
    fresh_values = noise(own_keys[5], (STEPS, D_KV), 1.0, 6.0)
    chosen = draw_chosen(jax.random.fold_in(jax.random.fold_in(streams_of[9], part), 71), part)
    shard_counts = draw_shard_counts(jax.random.fold_in(jax.random.fold_in(streams_of[9], part), 71), part)
    outliers = draw_outliers(jax.random.fold_in(jax.random.fold_in(streams_of[9], part), 71), part)
    return {"cache_keys": cache_keys, "cache_values": cache_values, "sketch_matrix": sketch_matrix, "queries": queries, "fresh_keys": fresh_keys, "fresh_values": fresh_values, "chosen": chosen, "shard_counts": shard_counts, "outliers": outliers}


def rotate(vectors, positions):
    half_width = vectors.shape[-1] // 2
    exponents = jnp.arange(half_width, dtype=jnp.float32) * (2.0 / vectors.shape[-1])
    inverse_freq = jnp.exp(-jnp.log(jnp.float32(500000.0)) * exponents)
    angles = positions.astype(jnp.float32)[..., None] * inverse_freq
    cosine = jnp.cos(angles)
    sine = jnp.sin(angles)
    first_half = vectors[..., :half_width]
    second_half = vectors[..., half_width:]
    return jnp.concatenate([first_half * cosine - second_half * sine, second_half * cosine + first_half * sine], axis=-1)

def make_basis(sketch):
    small_gram = jnp.dot(sketch.T, sketch, precision=lax.Precision.HIGHEST)
    lower = jnp.linalg.cholesky(small_gram)
    solved = lax.linalg.triangular_solve(lower, sketch.T, left_side=True, lower=True)
    return solved.T.astype(jnp.bfloat16)

def reference(cache_keys, cache_values, sketch_matrix, queries, fresh_keys, fresh_values, chosen, shard_counts, outliers):
    contract = (((0,), (0,)), ((), ()))
    gram_total = lax.dot_general(cache_keys.astype(jnp.float32), cache_keys.astype(jnp.float32), contract, preferred_element_type=jnp.float32) / LENGTH
    sketch = jnp.dot(gram_total, sketch_matrix, precision=lax.Precision.HIGHEST)
    key_basis = make_basis(sketch)
    key_factor = jnp.dot(cache_keys.astype(jnp.float32), key_basis.astype(jnp.float32), preferred_element_type=jnp.float32)
    preceding = jnp.cumsum(shard_counts, axis=2) - shard_counts
    padded_list = jnp.concatenate([chosen, jnp.zeros((STEPS, KVH, MOST), jnp.int32)], axis=2)
    slot_ids = jnp.arange(MOST, dtype=jnp.int32)
    place = (preceding[..., None] + slot_ids).reshape(STEPS, KVH, N_SEQ * MOST)
    picked = jnp.take_along_axis(padded_list, place, axis=2).reshape(STEPS, KVH, N_SEQ, MOST)
    is_live = slot_ids < shard_counts[..., None]
    shard_base = (jnp.arange(N_SEQ, dtype=jnp.int32) * CH_DEV)[:, None]
    span_ids = jnp.clip(picked - shard_base, 0, CH_DEV - 1) + shard_base
    span_ids = span_ids.reshape(STEPS, KVH, N_SEQ * MOST)
    is_live = is_live.reshape(STEPS, KVH, N_SEQ * MOST)
    factor_spans = key_factor.reshape(TOTAL_CH, SPAN, RANK)[span_ids]
    basis_heads = key_basis.reshape(KVH, HD, RANK)
    rebuilt = jnp.einsum('tgmcr,gdr->tgmcd', factor_spans.astype(jnp.float32), basis_heads.astype(jnp.float32), precision=lax.Precision.HIGHEST)
    token_pos = span_ids[..., None] * SPAN + jnp.arange(SPAN, dtype=jnp.int32)
    sel_keys = rotate(rebuilt, token_pos).astype(jnp.bfloat16)
    value_blocks = cache_values.reshape(TOTAL_CH, SPAN, KVH, HD)
    head_ids = jnp.arange(KVH, dtype=jnp.int32)
    sel_values = value_blocks[span_ids, :, head_ids[None, :, None], :]
    key_blocks = cache_keys.reshape(TOTAL_CH, SPAN, KVH, HD)
    out_keys = key_blocks[outliers[None, :], :, head_ids[:, None], :]
    out_pos = outliers[:, None] * SPAN + jnp.arange(SPAN, dtype=jnp.int32)
    out_keys = rotate(out_keys.astype(jnp.float32), out_pos).astype(jnp.bfloat16)
    out_values = value_blocks[outliers[None, :], :, head_ids[:, None], :]
    all_keys = jnp.concatenate([sel_keys.reshape(STEPS, KVH, -1, HD), jnp.broadcast_to(out_keys.reshape(1, KVH, -1, HD), (STEPS, KVH, OUTL * SPAN, HD))], axis=2)
    all_values = jnp.concatenate([sel_values.reshape(STEPS, KVH, -1, HD), jnp.broadcast_to(out_values.reshape(1, KVH, -1, HD), (STEPS, KVH, OUTL * SPAN, HD))], axis=2)
    live_tokens = jnp.concatenate([jnp.repeat(is_live, SPAN, axis=2), jnp.ones((STEPS, KVH, OUTL * SPAN), bool)], axis=2)
    step_pos = LENGTH + jnp.arange(STEPS, dtype=jnp.int32)
    query_rows = rotate(queries.reshape(STEPS, QH, HD).astype(jnp.float32), step_pos[:, None]).reshape(STEPS, KVH, GROUP, HD)
    new_keys = rotate(fresh_keys.reshape(STEPS, KVH, HD).astype(jnp.float32), step_pos[:, None]).astype(jnp.bfloat16)
    new_values = fresh_values.reshape(STEPS, KVH, HD)
    score_scale = 1.0 / jnp.sqrt(jnp.float32(HD))
    cache_scores = jnp.einsum('tgqd,tgld->tgql', query_rows, all_keys.astype(jnp.float32), precision=lax.Precision.HIGHEST) * score_scale
    cache_scores = jnp.where(live_tokens[:, :, None, :], cache_scores, -1e+30)
    new_scores = jnp.einsum('tgqd,sgd->tgqs', query_rows, new_keys.astype(jnp.float32), precision=lax.Precision.HIGHEST) * score_scale
    causal = jnp.arange(STEPS)[None, :] <= jnp.arange(STEPS)[:, None]
    new_scores = jnp.where(causal[:, None, None, :], new_scores, -1e+30)
    row_max = jnp.maximum(lax.optimization_barrier(jnp.max(cache_scores, axis=-1)), lax.optimization_barrier(jnp.max(new_scores, axis=-1)))
    cache_weights = jnp.exp(cache_scores - row_max[..., None]) * live_tokens[:, :, None, :]
    new_weights = jnp.exp(new_scores - row_max[..., None]) * causal[:, None, None, :]
    totals = lax.optimization_barrier(jnp.sum(cache_weights, axis=-1)) + lax.optimization_barrier(jnp.sum(new_weights, axis=-1))
    summed = jnp.einsum('tgql,tgld->tgqd', cache_weights, all_values.astype(jnp.float32), precision=lax.Precision.HIGHEST)
    summed = summed + jnp.einsum('tgqs,sgd->tgqd', new_weights, new_values.astype(jnp.float32), precision=lax.Precision.HIGHEST)
    attended = (summed / totals[..., None]).reshape(STEPS, QH * HD).astype(jnp.bfloat16)
    return (attended, key_factor)
```

```python
import functools

import jax
import jax.numpy as jnp
import numpy as np
from jax import lax
from jax.experimental import pallas as pl
from jax.experimental.pallas import tpu as pltpu
from jax.sharding import PartitionSpec as P

KVH = 8
HD = 128
QH = 64
SPAN = 8
OMOST = 4
GROUP = QH // KVH
HALF = HD // 2
LANES = 128
CHUNK = 1024
TILES = CHUNK // LANES
PAIRS = KVH // 2
THETA = 500000.0
DEAD = -1e30
VMEM_LIMIT = 60 * 1024 * 1024
MESH = pl.DeviceIdType.MESH
HIGHEST = lax.Precision.HIGHEST
NT = (((1,), (1,)), ((), ()))
NN = (((1,), (0,)), ((), ()))
F32 = jnp.float32
BF16 = jnp.bfloat16


def dot(a, b, dims=NN, precision=None):
    return lax.dot_general(a, b, dims, precision=precision, preferred_element_type=F32)


def pieces(x, count):
    parts = []
    for _ in range(count):
        part = x.astype(BF16)
        parts.append(part)
        x = x - part.astype(F32)
    return parts


def iota(shape, axis):
    return lax.broadcasted_iota(jnp.int32, shape, axis)


def vmem(shape=None, index=None):
    if shape is None:
        return pl.BlockSpec(memory_space=pltpu.VMEM)
    return pl.BlockSpec(shape, index)


def remote(src, dst, send, recv, target):
    return pltpu.make_async_remote_copy(
        src_ref=src, dst_ref=dst, send_sem=send, recv_sem=recv,
        device_id=target, device_id_type=MESH,
    )


def eliminate(m_ref, rank):
    wide = m_ref.shape[1] // 2
    block = 32
    for top in range(0, rank, block):
        low = top + block
        starts = [c for c in range(0, wide, LANES) if c + LANES > top]
        starts += [wide + c for c in range(0, wide, LANES) if c < low]
        tiles = [m_ref[top:low, c : c + LANES] for c in starts]
        pivots = []
        for j in range(0, block, 8):
            at = top + j
            source = tiles[starts.index(at // LANES * LANES)]
            parts = [t[j:] for t in tiles]
            height = block - j
            columns = [
                jnp.broadcast_to(source[j:, at % LANES + k : at % LANES + k + 1], (height, LANES))
                for k in range(8)
            ]
            row = iota((height, LANES), 0)
            row8 = iota((8, LANES), 0)
            diagonal = jnp.ones((8, LANES), F32)
            for k in range(8):
                pivot = columns[k][k : k + 1, :]
                inverse = 1.0 / pivot
                for m in range(k + 1, 8):
                    columns[m] = columns[m] - (columns[k] * columns[m][k : k + 1, :]) * inverse
                factor = jnp.where(row > k, columns[k] * inverse, 0.0)
                diagonal = jnp.where(row8 == k, pivot, diagonal)
                parts = [t - factor * t[k : k + 1, :] for t in parts]
            pivots.append(diagonal)
            tiles = [
                jnp.concatenate([t[:j], p], axis=0) if j else p for t, p in zip(tiles, parts)
            ]
        scale = 1.0 / jnp.sqrt(jnp.concatenate(pivots, axis=0))
        tiles = [t * scale for t in tiles]
        for c, t in zip(starts, tiles):
            m_ref[top:low, c : c + LANES] = t
        if low < rank:
            a = jnp.concatenate([t for c, t in zip(starts, tiles) if c < wide], axis=1)
            a_t = a.T[low - starts[0] : rank - starts[0], :]
            for c, t in zip(starts, tiles):
                m_ref[low:rank, c : c + LANES] -= dot(a_t, t, NN, HIGHEST)


def basis_kernel(
    devices, length, steps, outl, s_ref, k_hbm, q_ref, fk_ref, fv_ref, chosen_ref, cosq_ref,
    sinq_ref, ang_hbm,
    b_out, bt_out, qb_out, bias_out, init_out, ang_out,
    kbuf, terms, coords, mine, crossed, sbuf, own32, inbox, full, sketch, m_ref, qrows, live,
    ang_land, k_sem, cross_s, cross_r, rs_s, rs_r, ag_s, ag_r, fwd_s, fwd_r, ang_sem,
):
    chips = devices // 2
    rank, width = s_ref.shape
    half = rank // 2
    regions = width // (2 * LANES)
    per = chips // regions
    split = per // 2
    block_rows = full.shape[2]
    me = lax.axis_index("seq")
    core = lax.rem(me, 2)
    other = 1 - core
    chip = me // 2
    region = chip // per
    place = lax.rem(chip, per)
    partner = {"seq": chip * 2 + other}
    seq_len = k_hbm.shape[0]
    chunks = seq_len // CHUNK
    spans = seq_len // SPAN
    base = me * spans

    pair, bit = region // 2, lax.rem(region, 2)

    def shifted(far):
        return lax.rem(pair + far // 2, 2) * 2 + lax.rem(bit + far % 2, 2)

    def neighbour(sid):
        q = shifted(sid // per) * per + lax.rem(place + sid % per, per)
        return {"seq": q * 2 + core}

    def source_chip(sid):
        return shifted(sid // per) * per + lax.rem(place + per - sid % per, per)

    fetch = []
    for i in range(chunks):
        rows = pl.ds(i * CHUNK, CHUNK)
        copy = pltpu.make_async_copy(k_hbm.at[rows, :], kbuf.at[rows, :], k_sem.at[i])
        copy.start()
        fetch.append(copy)
    ang_copy = pltpu.make_async_copy(ang_hbm.at[me], ang_land, ang_sem)
    ang_copy.start()
    barrier = pltpu.get_barrier_semaphore()
    pl.semaphore_signal(barrier, inc=1, device_id=partner, device_id_type=MESH)
    for sid in range(1, chips):
        pl.semaphore_signal(barrier, inc=1, device_id=neighbour(sid), device_id_type=MESH)

    for i, part in enumerate(pieces(s_ref[...], 2)):
        terms[i * rank : (i + 1) * rank, :] = part
    for i in range(chunks):
        fetch[i].wait()
        wide = dot(terms[...], kbuf[i * CHUNK : (i + 1) * CHUNK, :], NT)
        coords[:, i * CHUNK : (i + 1) * CHUNK] = (wide[:rank] + wide[rank:]).astype(BF16)
    pl.semaphore_wait(barrier, chips)

    crossing = {}
    sent = {}

    def produce(which):
        target = lax.rem(pair + which, 2)
        columns = pl.ds(pl.multiple_of(target * 4 * LANES, 4 * LANES), 4 * LANES)
        share = dot(coords[...], kbuf[:, columns]) / length
        for low in (1, 0):
            far = 2 * which + low
            part = jnp.where(
                lax.rem(bit + low, 2) == 0, share[:, : 2 * LANES], share[:, 2 * LANES :]
            )
            mine[far, 0] = jnp.where(core == 0, part[:half], part[half:])
            mine[far, 1] = jnp.where(core == 0, part[half:], part[:half])
            crossing[far] = remote(
                mine.at[far, 1], crossed.at[far], cross_s.at[far], cross_r.at[far], partner
            )
            crossing[far].start()

    def deliver(far):
        crossing[far].wait_recv()
        both = mine[far, 0] + crossed[far]
        for index in range(per):
            tile, part = index // split, index % split
            piece = both[:, tile * LANES : (tile + 1) * LANES]
            rows = piece[part * block_rows : (part + 1) * block_rows]
            if rows.shape[0] < block_rows:
                rows = jnp.concatenate(
                    [rows, jnp.zeros((block_rows - rows.shape[0], LANES), F32)], axis=0
                )
            if far == 0:
                own32[index] = rows
            sbuf[far, index] = rows.astype(BF16)
        for near in range(1 if far == 0 else 0, per):
            sid = far * per + near
            sent[sid] = remote(
                sbuf.at[far, lax.rem(place + near, per)], inbox.at[sid], rs_s.at[sid],
                rs_r.at[sid], neighbour(sid),
            )
            sent[sid].start()

    order = (3, 2, 1, 0)
    produce(1)
    deliver(3)
    deliver(2)
    produce(0)
    deliver(1)
    deliver(0)

    lists = steps * KVH
    listed = chosen_ref[...] - base
    tile_of = listed >> 7
    lane_of = (listed & (LANES - 1)).astype(F32).T
    span_id = iota((8, spans), 1)
    out_row = jnp.zeros((8, spans), F32)
    for i in range(outl.shape[0]):
        out_row = jnp.where(span_id == outl[i] - base, 1.0, out_row)
    count = listed.shape[1]
    lane_id = iota((count, LANES), 1).astype(F32)
    tile_id = iota((8, count), 0)
    for i in range(lists):
        right = jnp.where(lane_of[:, i : i + 1] == lane_id, 1.0, 0.0).astype(BF16)
        left = jnp.where(tile_of[i : i + 1, :] == tile_id, 1.0, 0.0).astype(BF16)
        found = dot(left, right)
        for c in range(spans // LANES):
            here = slice(c * LANES, (c + 1) * LANES)
            live[i : i + 1, here] = jnp.maximum(found[c : c + 1], out_row[:1, here])
    rows_all = steps * QH
    at_row = iota((rows_all, lists), 0)
    wanted = at_row % steps * KVH + at_row // (steps * GROUP)
    widen = jnp.where(iota((rows_all, lists), 1) == wanted, 1.0, 0.0).astype(BF16)
    bias_out[...] = ((1.0 - dot(widen, live[...].astype(BF16))) * DEAD).astype(BF16)

    total = own32[place]
    for sid in range(1, chips):
        sent[sid].wait_recv()
        total = total + inbox[sid].astype(F32)
    full[core, chip] = total.astype(BF16)
    back = {}
    for sid in [far * per + near for far in order for near in range(per)]:
        if sid:
            back[sid] = remote(
                full.at[core, chip], full.at[core, chip], ag_s.at[sid], ag_r.at[sid],
                neighbour(sid),
            )
            back[sid].start()
    forward = {}
    forward[0] = remote(
        full.at[core, chip], full.at[core, chip], fwd_s.at[0], fwd_r.at[0], partner
    )
    forward[0].start()

    scale = 1.0 / (HD ** 0.5)
    cosq = cosq_ref[:steps, :]
    sinq = sinq_ref[:steps, :]

    def rope(x):
        return x * cosq + pltpu.roll(x, HALF, 1) * sinq

    for h in range(QH):
        x = q_ref[:, h * HD : (h + 1) * HD].astype(F32) * scale
        qrows[h * steps : (h + 1) * steps, :] = rope(x)
    list_rows = steps * GROUP
    lane = iota((list_rows, 8), 1)
    step_of = iota((list_rows, 8), 0) % steps
    reach = jnp.where(me == 0, 0, -steps)
    allowed = lane <= step_of + reach
    pad = jnp.zeros((8 - steps, HD), F32)
    zeros = jnp.zeros((list_rows, HD), F32)
    for g in range(KVH):
        columns = slice(g * HD, (g + 1) * HD)
        rows = slice(g * list_rows, (g + 1) * list_rows)
        q = qrows[rows, :]
        side = [q, zeros] if g % 2 == 0 else [zeros, q]
        at = g % 2 * list_rows
        qb_out[g // 2, at : at + list_rows, :] = jnp.concatenate(side, axis=1).astype(BF16)
        keys = rope(fk_ref[:, columns].astype(F32)).astype(BF16).astype(F32)
        keys = jnp.concatenate([keys, pad], axis=0)
        values = jnp.concatenate([fv_ref[:, columns].astype(F32), pad], axis=0)
        scores = jnp.where(allowed, dot(q, keys, NT, HIGHEST), DEAD)
        top = jnp.max(scores, axis=1, keepdims=True)
        weights = jnp.where(allowed, jnp.exp(scores - top), 0.0)
        init_out[0, rows, :] = dot(weights, values, NN, HIGHEST)
        init_out[1, rows, :] = jnp.broadcast_to(top, (list_rows, LANES))
        init_out[2, rows, :] = jnp.broadcast_to(
            jnp.sum(weights, axis=1, keepdims=True), (list_rows, LANES)
        )
    ang_copy.wait()
    for i in range(chunks):
        ang_out[i] = jnp.concatenate(
            [ang_land[:, i * 2 * TILES : (i + 1) * 2 * TILES]]
            + [jnp.zeros((HALF, LANES - 2 * TILES), F32)], axis=1
        )

    for sid in range(1, chips):
        source = source_chip(sid)
        remote(
            full.at[core, source], full.at[core, source], ag_s.at[sid], ag_r.at[sid],
            neighbour(sid),
        ).wait_recv()
        forward[sid] = remote(
            full.at[core, source], full.at[core, source], fwd_s.at[sid], fwd_r.at[sid], partner
        )
        forward[sid].start()
    for sid in range(chips):
        source = source_chip(sid)
        remote(
            full.at[other, source], full.at[other, source], fwd_s.at[sid], fwd_r.at[sid], partner
        ).wait_recv()
    for k in range(2):
        for q in range(chips):
            tile, part = q // split, q % split
            top = part * block_rows
            count = min(block_rows, half - top)
            sketch[k * half + top : k * half + top + count, tile * LANES : (tile + 1) * LANES] = (
                full[k, q, :count]
            )

    sk = sketch[...]
    gram = dot(sk, sk, NT)
    wide = m_ref.shape[1] // 2
    m_ref[...] = jnp.zeros_like(m_ref)
    m_ref[:, :rank] = gram
    m_ref[:, wide : wide + rank] = jnp.where(
        iota((rank, rank), 0) == iota((rank, rank), 1), 1.0, 0.0
    )
    eliminate(m_ref, rank)
    inverse = pieces(m_ref[:, wide : wide + rank], 3)
    basis = dot(inverse[0], sk) + dot(inverse[1], sk) + dot(inverse[2], sk)
    b_out[...] = basis.astype(BF16)
    bt_out[...] = basis.astype(BF16).T

    for far in range(regions):
        crossing[far].wait_send()
    for sid in range(chips):
        forward[sid].wait_send()
        if sid:
            sent[sid].wait_send()
            back[sid].wait_send()


def make_basis(s_t, cache_keys, queries, fresh_k, fresh_v, chosen, outliers, tables, devices):
    cosq, sinq, ang = tables
    rank, width = s_t.shape
    seq_len = cache_keys.shape[0]
    length = seq_len * devices
    steps = queries.shape[0]
    chips = devices // 2
    regions = width // (2 * LANES)
    per = chips // regions
    split = per // 2
    groups16 = rank // 2 // 16
    block_rows = 16 * (-(-groups16 // split))
    rows = steps * QH
    wide = -(-rank // LANES) * LANES
    spans = seq_len // SPAN
    dma = lambda *n: pltpu.SemaphoreType.DMA(n)
    anywhere = pl.BlockSpec(memory_space=pl.ANY)
    shape = jax.ShapeDtypeStruct
    block = (block_rows, LANES)
    return pl.pallas_call(
        functools.partial(basis_kernel, devices, length, steps),
        out_shape=(
            shape((rank, width), BF16),
            shape((width, rank), BF16),
            shape((PAIRS, rows // PAIRS, 2 * HD), BF16),
            shape((rows, spans), BF16),
            shape((3, rows, LANES), F32),
            shape((seq_len // CHUNK,) + ang.shape[1:], F32),
        ),
        in_specs=[
            pl.BlockSpec(memory_space=pltpu.SMEM), vmem(), anywhere, vmem(), vmem(), vmem(), vmem(),
            vmem(), vmem(), anywhere,
        ],
        out_specs=(vmem(),) * 6,
        scratch_shapes=[
            pltpu.VMEM(cache_keys.shape, BF16),
            pltpu.VMEM((2 * rank, width), BF16),
            pltpu.VMEM((rank, seq_len), BF16),
            pltpu.VMEM((regions, 2, rank // 2, 2 * LANES), F32),
            pltpu.VMEM((regions, rank // 2, 2 * LANES), F32),
            pltpu.VMEM((regions, per) + block, BF16),
            pltpu.VMEM((per,) + block, F32),
            pltpu.VMEM((chips,) + block, BF16),
            pltpu.VMEM((2, chips) + block, BF16),
            pltpu.VMEM((rank, width), BF16),
            pltpu.VMEM((rank, 2 * wide), F32),
            pltpu.VMEM((rows, HD), F32),
            pltpu.VMEM((steps * KVH, spans), F32),
            pltpu.VMEM(ang.shape[1:], F32),
            dma(seq_len // CHUNK), dma(regions), dma(regions), dma(chips), dma(chips), dma(chips),
            dma(chips), dma(chips), dma(chips), pltpu.SemaphoreType.DMA,
        ],
        compiler_params=pltpu.CompilerParams(
            collective_id=0, has_side_effects=True, vmem_limit_bytes=VMEM_LIMIT
        ),
        name="key_basis",
    )(
        outliers, s_t, cache_keys, queries, fresh_k, fresh_v, chosen, cosq, sinq, ang,
    )


def attend_kernel(
    devices, outl, k_ref, v_ref, k_all, b_ref, bt_ref, qb_ref, bias_ref, init_ref, ang_ref,
    fine_ref, factor_ref, deal_ref, bx_ref, pos_ref, land, rhs, turn, keys, out, top, total, sems,
):
    step = pl.program_id(0)
    rank = b_ref.shape[0]
    rows = qb_ref.shape[1]
    half_rows = rows // 2

    @pl.when(step == 0)
    def _():
        spans = k_all.shape[0] // SPAN
        base = lax.axis_index("seq") * spans
        last = outl.shape[0] - 1
        before = jnp.int32(0)
        for i in range(outl.shape[0]):
            before = before + (outl[i] < base).astype(jnp.int32)
        place = iota((OMOST * SPAN, LANES), 0)
        target = jnp.full((OMOST * SPAN, LANES), -1, jnp.int32)
        copies = []
        for j in range(OMOST):
            index = before + j
            span = outl[jnp.minimum(index, last)] - base
            valid = (index <= last) & (span >= 0) & (span < spans)
            at = jnp.where(valid, span, 0)
            copy = pltpu.make_async_copy(
                k_all.at[pl.ds(pl.multiple_of(at * SPAN, SPAN), SPAN), :], land.at[j], sems.at[j]
            )
            copy.start()
            copies.append(copy)
            spot = jnp.where(valid, (at - j) * SPAN, -LANES * SPAN)
            target = jnp.where((place // SPAN == j) & (place + spot >= 0), place + spot, target)
        pos_ref[...] = target
        bx_ref[:, :rank] = bt_ref[...]
        out[...] = init_ref[0]
        top[...] = init_ref[1]
        total[...] = init_ref[2]
        token = iota((LANES, CHUNK), 1)
        spread = jnp.where(token // SPAN == iota((LANES, CHUNK), 0), 1.0, 0.0).astype(BF16)
        for p in range(PAIRS):
            keys[p, 2 * HD :, :] = spread
        for copy in copies:
            copy.wait()
        exact = jnp.concatenate([land[j].astype(F32) for j in range(OMOST)], axis=0)
        bx_ref[:, rank:] = exact.T.astype(BF16)

    cb, sb = fine_ref[0], fine_ref[1]
    ang = ang_ref[0]
    for i in range(TILES):
        here = slice(i * LANES, (i + 1) * LANES)
        ca, sa = ang[:, i : i + 1], ang[:, TILES + i : TILES + i + 1]
        turn[:HALF, here] = ca * cb - sa * sb
        turn[HALF:, here] = sa * cb + ca * sb

    factor = dot(b_ref[...], k_ref[...], NT)
    factor_ref[...] = factor
    lane = iota((pos_ref.shape[0], LANES), 1) + step * CHUNK
    for i in range(TILES):
        here = slice(i * LANES, (i + 1) * LANES)
        exact = jnp.where(pos_ref[...] == lane + i * LANES, 1.0, 0.0)
        rhs[rank:, here] = exact.astype(BF16)
        keep = 1.0 - jnp.sum(exact, axis=0, keepdims=True)
        rhs[:rank, here] = (factor[:, here] * keep).astype(BF16)

    def rebuild(first_head, heads, tokens):
        x = dot(bx_ref[first_head * HD : (first_head + heads) * HD, :], rhs[:, tokens])
        cosine, sine = turn[:HALF, tokens], turn[HALF:, tokens]
        for n in range(heads):
            head = first_head + n
            one, two = x[n * HD : n * HD + HALF], x[n * HD + HALF : (n + 1) * HD]
            p, at = head // 2, head % 2 * HD
            keys[p, at : at + HALF, tokens] = (one * cosine - two * sine).astype(BF16)
            keys[p, at + HALF : at + HD, tokens] = (two * cosine + one * sine).astype(BF16)

    def absorb(p, tokens):
        here = slice(p * rows, (p + 1) * rows)
        left = jnp.concatenate([qb_ref[p], bias_ref[here, :]], axis=1)
        scores = dot(left, keys[p, :, tokens])
        before = top[here, :]
        after = jnp.maximum(before, jnp.max(scores, axis=1, keepdims=True))
        weights = jnp.exp(scores - after[:, :1])
        scale = jnp.exp(before - after)
        top[here, :] = after
        total[here, :] = total[here, :] * scale + jnp.sum(weights, axis=1, keepdims=True)
        both = dot(weights.astype(BF16), v_ref[tokens, p * 2 * HD : (p + 1) * 2 * HD])
        own = jnp.concatenate([both[:half_rows, :HD], both[half_rows:, HD:]], axis=0)
        out[here, :] = out[here, :] * scale + own

    parts = [slice(t, t + 512) for t in range(0, CHUNK, 512)]
    for tokens in parts:
        for h in range(0, KVH, 8):
            rebuild(h, 8, tokens)
    for p in range(PAIRS):
        absorb(p, slice(0, CHUNK))

    @pl.when(step == pl.num_programs(0) - 1)
    def _():
        each = out.shape[0] // devices
        sums = total[...]
        mean = out[...] / jnp.where(sums > 0.0, sums, 1.0)
        level = jnp.where(sums > 0.0, top[...] + jnp.log(jnp.where(sums > 0.0, sums, 1.0)), DEAD)
        owner = iota((devices, out.shape[0]), 1) // each == iota((devices, out.shape[0]), 0)
        gather = jnp.where(owner, 1.0, 0.0).astype(BF16)
        spot = iota(level.shape, 0) % each == iota(level.shape, 1)
        level = [dot(gather, part) for part in pieces(jnp.where(spot, level, 0.0), 3)]
        rest = jnp.zeros((16 - each - 3, LANES), F32)
        for d in range(devices):
            here = slice(d * each, (d + 1) * each)
            deal_ref[d] = jnp.concatenate(
                [mean[here]] + [part[d : d + 1] for part in level] + [rest], axis=0
            ).astype(BF16)


def attend(cache_keys, cache_values, outliers, made, fine, devices):
    basis, bt, qb, bias, init, ang = made
    seq_len, width = cache_keys.shape
    rank = basis.shape[0]
    rows = init.shape[1]
    whole = lambda x: vmem(x.shape, lambda i: (0,) * len(x.shape))
    deal = (devices, 16, LANES)
    exact = OMOST * SPAN
    return pl.pallas_call(
        functools.partial(attend_kernel, devices),
        grid=(seq_len // CHUNK,),
        out_shape=(
            jax.ShapeDtypeStruct((rank, seq_len), F32),
            jax.ShapeDtypeStruct(deal, BF16),
        ),
        in_specs=[
            pl.BlockSpec(memory_space=pltpu.SMEM),
            vmem((CHUNK, width), lambda i: (i, 0)),
            vmem((CHUNK, width), lambda i: (i, 0)),
            pl.BlockSpec(memory_space=pl.ANY),
            whole(basis), whole(bt), whole(qb),
            vmem((rows, LANES), lambda i: (0, i)),
            whole(init),
            vmem((1,) + ang.shape[1:], lambda i: (i, 0, 0)),
            whole(fine),
        ],
        out_specs=(
            vmem((rank, CHUNK), lambda i: (0, i)),
            vmem(deal, lambda i: (0, 0, 0)),
        ),
        scratch_shapes=[
            pltpu.VMEM((width, rank + exact), BF16),
            pltpu.VMEM((exact, LANES), jnp.int32),
            pltpu.VMEM((OMOST, SPAN, width), BF16),
            pltpu.VMEM((rank + exact, CHUNK), BF16),
            pltpu.VMEM((HD, CHUNK), F32),
            pltpu.VMEM((PAIRS, 2 * HD + LANES, CHUNK), BF16),
            pltpu.VMEM((rows, LANES), F32),
            pltpu.VMEM((rows, LANES), F32),
            pltpu.VMEM((rows, LANES), F32),
            pltpu.SemaphoreType.DMA((OMOST,)),
        ],
        compiler_params=pltpu.CompilerParams(
            vmem_limit_bytes=VMEM_LIMIT
        ),
        name="attend",
    )(outliers, cache_keys, cache_values, cache_keys, basis, bt, qb, bias, init, ang, fine)


def merge_kernel(devices, x_ref, out_ref, inbox, send_sem, recv_sem):
    me = lax.axis_index("seq")
    steps = out_ref.shape[0]
    heads = out_ref.shape[1] // HD
    rows = steps * heads

    def peer(off):
        return lax.rem(me + off, devices)

    barrier = pltpu.get_barrier_semaphore()
    for off in range(1, devices):
        pl.semaphore_signal(
            barrier, inc=1, device_id={"seq": peer(off)}, device_id_type=MESH
        )
    pl.semaphore_wait(barrier, devices - 1)
    copies = []
    for off in range(1, devices):
        copy = remote(
            x_ref.at[peer(off)], inbox.at[off], send_sem.at[off], recv_sem.at[off],
            {"seq": peer(off)},
        )
        copy.start()
        copies.append(copy)
    own = x_ref[me]
    spot = iota((rows, LANES), 1) == iota((rows, LANES), 0)

    def unpack(block):
        block = block.astype(F32)
        level = block[rows : rows + 1] + block[rows + 1 : rows + 2] + block[rows + 2 : rows + 3]
        level = jnp.sum(jnp.where(spot, level, 0.0), axis=1, keepdims=True)
        return block[:rows], level

    blocks = [unpack(own)]
    for off, copy in enumerate(copies):
        copy.wait_recv()
        blocks.append(unpack(inbox[off + 1]))
    joint = functools.reduce(jnp.maximum, [level for _, level in blocks])
    total = jnp.zeros((rows, 1), F32)
    summed = jnp.zeros((rows, HD), F32)
    for block, level in blocks:
        scale = jnp.exp(level - joint)
        total = total + scale
        summed = summed + block * scale
    result = summed / total
    for h in range(heads):
        out_ref[:, h * HD : (h + 1) * HD] = result[h * steps : (h + 1) * steps].astype(
            out_ref.dtype
        )
    for copy in copies:
        copy.wait_send()


def merge(x, steps):
    devices = x.shape[0]
    return pl.pallas_call(
        functools.partial(merge_kernel, devices),
        out_shape=jax.ShapeDtypeStruct((steps, QH // devices * HD), BF16),
        in_specs=[vmem()],
        out_specs=vmem(),
        scratch_shapes=[
            pltpu.VMEM(x.shape, BF16),
            pltpu.SemaphoreType.DMA((devices,)),
            pltpu.SemaphoreType.DMA((devices,)),
        ],
        compiler_params=pltpu.CompilerParams(collective_id=1, has_side_effects=True),
        name="merge",
    )(x)


def rotation_tables(seq_len, devices, steps):
    freq = np.exp(-np.log(THETA) * np.arange(HALF) * (2.0 / HD))
    fine = np.arange(LANES)[None, :] * freq[:, None]
    fine = np.stack([np.cos(fine), np.sin(fine)]).astype(np.float32)
    coarse = np.arange(seq_len * devices // LANES).reshape(devices, -1, 1, TILES) * LANES
    coarse = coarse * freq[:, None]
    coarse = np.concatenate([np.cos(coarse), np.sin(coarse)], axis=3)
    ang = np.zeros((devices, HALF, LANES), np.float32)
    ang[:, :, : coarse.shape[1] * 2 * TILES] = np.moveaxis(coarse, 1, 2).reshape(
        devices, HALF, -1
    )
    decoded = (seq_len * devices + np.arange(8))[:, None] * freq
    cosq = np.concatenate([np.cos(decoded)] * 2, axis=1).astype(np.float32)
    sinq = np.concatenate([-np.sin(decoded), np.sin(decoded)], axis=1).astype(np.float32)
    return fine, ang, cosq, sinq


def on_device(
    cache_keys,
    cache_values,
    sketch_matrix,
    queries,
    fresh_keys,
    fresh_values,
    chosen,
    shard_counts,
    outliers,
):
    devices = lax.axis_size("seq")
    steps = queries.shape[0]
    fine, ang, cosq, sinq = rotation_tables(cache_keys.shape[0], devices, steps)
    made = make_basis(
        sketch_matrix.T, cache_keys, queries, fresh_keys, fresh_values,
        chosen.reshape(steps * KVH, chosen.shape[2]), outliers, (cosq, sinq, ang), devices,
    )
    factor_t, parts = attend(cache_keys, cache_values, outliers, made, fine, devices)
    return (merge(parts, steps), factor_t.T)


def solution(mesh):
    in_specs = (
        P(("groups", "seq"), None),
        P(("groups", "seq"), None),
        P(),
        P("groups", None),
        P("groups", None),
        P("groups", None),
        P("groups", None, None),
        P("groups", None, None),
        P("groups"),
    )
    out_specs = (P("groups", "seq"), P(("groups", "seq"), None))
    return jax.shard_map(
        on_device, mesh=mesh, in_specs=in_specs, out_specs=out_specs, check_vma=False
    )
```

```python
import functools

import jax
import jax.numpy as jnp
import numpy as np
from jax import lax
from jax.experimental import pallas as pl
from jax.experimental.pallas import tpu as pltpu
from jax.sharding import PartitionSpec as P

KVH = 8
HD = 128
QH = 64
SPAN = 8
OMOST = 4
GROUP = QH // KVH
HALF = HD // 2
LANES = 128
CHUNK = 1024
TILES = CHUNK // LANES
PAIRS = KVH // 2
THETA = 500000.0
DEAD = -1e30
VMEM_LIMIT = 60 * 1024 * 1024
MESH = pl.DeviceIdType.MESH
HIGHEST = lax.Precision.HIGHEST
NT = (((1,), (1,)), ((), ()))
NN = (((1,), (0,)), ((), ()))
F32 = jnp.float32
BF16 = jnp.bfloat16


def dot(a, b, dims=NN, precision=None):
    return lax.dot_general(a, b, dims, precision=precision, preferred_element_type=F32)


def pieces(x, count):
    parts = []
    for _ in range(count):
        part = x.astype(BF16)
        parts.append(part)
        x = x - part.astype(F32)
    return parts


def iota(shape, axis):
    return lax.broadcasted_iota(jnp.int32, shape, axis)


def vmem(shape=None, index=None):
    if shape is None:
        return pl.BlockSpec(memory_space=pltpu.VMEM)
    return pl.BlockSpec(shape, index)


def remote(src, dst, send, recv, target):
    return pltpu.make_async_remote_copy(
        src_ref=src, dst_ref=dst, send_sem=send, recv_sem=recv,
        device_id=target, device_id_type=MESH,
    )


def eliminate(m_ref, rank):
    wide = m_ref.shape[1] // 2
    block = 32
    for top in range(0, rank, block):
        low = top + block
        starts = [c for c in range(0, wide, LANES) if c + LANES > top]
        starts += [wide + c for c in range(0, wide, LANES) if c < low]
        tiles = [m_ref[top:low, c : c + LANES] for c in starts]
        pivots = []
        for j in range(0, block, 8):
            at = top + j
            source = tiles[starts.index(at // LANES * LANES)]
            parts = [t[j:] for t in tiles]
            height = block - j
            columns = [
                jnp.broadcast_to(source[j:, at % LANES + k : at % LANES + k + 1], (height, LANES))
                for k in range(8)
            ]
            row = iota((height, LANES), 0)
            row8 = iota((8, LANES), 0)
            diagonal = jnp.ones((8, LANES), F32)
            for k in range(8):
                pivot = columns[k][k : k + 1, :]
                inverse = 1.0 / pivot
                for m in range(k + 1, 8):
                    columns[m] = columns[m] - (columns[k] * columns[m][k : k + 1, :]) * inverse
                factor = jnp.where(row > k, columns[k] * inverse, 0.0)
                diagonal = jnp.where(row8 == k, pivot, diagonal)
                parts = [t - factor * t[k : k + 1, :] for t in parts]
            pivots.append(diagonal)
            tiles = [
                jnp.concatenate([t[:j], p], axis=0) if j else p for t, p in zip(tiles, parts)
            ]
        scale = 1.0 / jnp.sqrt(jnp.concatenate(pivots, axis=0))
        tiles = [t * scale for t in tiles]
        for c, t in zip(starts, tiles):
            m_ref[top:low, c : c + LANES] = t
        if low < rank:
            a = jnp.concatenate([t for c, t in zip(starts, tiles) if c < wide], axis=1)
            a_t = a.T[low - starts[0] : rank - starts[0], :]
            for c, t in zip(starts, tiles):
                m_ref[low:rank, c : c + LANES] -= dot(a_t, t, NN, HIGHEST)


def basis_kernel(
    devices, length, steps, outl, s_ref, k_hbm, q_ref, fk_ref, fv_ref, chosen_ref, cosq_ref,
    sinq_ref, ang_hbm,
    b_out, bt_out, qb_out, bias_out, init_out, ang_out,
    kbuf, terms, coords, mine, crossed, sbuf, own32, inbox, full, sketch, m_ref, qrows, live,
    ang_land, k_sem, cross_s, cross_r, rs_s, rs_r, ag_s, ag_r, fwd_s, fwd_r, ang_sem,
):
    chips = devices // 2
    rank, width = s_ref.shape
    half = rank // 2
    regions = width // (2 * LANES)
    per = chips // regions
    split = per // 2
    block_rows = full.shape[2]
    me = lax.axis_index("seq")
    core = lax.rem(me, 2)
    other = 1 - core
    chip = me // 2
    region = chip // per
    place = lax.rem(chip, per)
    partner = {"seq": chip * 2 + other}
    seq_len = k_hbm.shape[0]
    chunks = seq_len // CHUNK
    spans = seq_len // SPAN
    base = me * spans

    pair, bit = region // 2, lax.rem(region, 2)

    def shifted(far):
        return lax.rem(pair + far // 2, 2) * 2 + lax.rem(bit + far % 2, 2)

    def neighbour(sid):
        q = shifted(sid // per) * per + lax.rem(place + sid % per, per)
        return {"seq": q * 2 + core}

    def source_chip(sid):
        return shifted(sid // per) * per + lax.rem(place + per - sid % per, per)

    fetch = []
    for i in range(chunks):
        rows = pl.ds(i * CHUNK, CHUNK)
        copy = pltpu.make_async_copy(k_hbm.at[rows, :], kbuf.at[rows, :], k_sem.at[i])
        copy.start()
        fetch.append(copy)
    ang_copy = pltpu.make_async_copy(ang_hbm.at[me], ang_land, ang_sem)
    ang_copy.start()
    barrier = pltpu.get_barrier_semaphore()
    pl.semaphore_signal(barrier, inc=1, device_id=partner, device_id_type=MESH)
    for sid in range(1, chips):
        pl.semaphore_signal(barrier, inc=1, device_id=neighbour(sid), device_id_type=MESH)

    terms[...] = s_ref[...].astype(BF16)
    for i in range(chunks):
        fetch[i].wait()
        here = slice(i * CHUNK, (i + 1) * CHUNK)
        coords[:, here] = dot(terms[...], kbuf[here, :], NT).astype(BF16)
    pl.semaphore_wait(barrier, chips)

    crossing = {}
    sent = {}

    def produce(which):
        target = lax.rem(pair + which, 2)
        columns = pl.ds(pl.multiple_of(target * 4 * LANES, 4 * LANES), 4 * LANES)
        share = dot(coords[...], kbuf[:, columns]) / length
        for low in (1, 0):
            far = 2 * which + low
            part = jnp.where(
                lax.rem(bit + low, 2) == 0, share[:, : 2 * LANES], share[:, 2 * LANES :]
            )
            mine[far, 0] = jnp.where(core == 0, part[:half], part[half:])
            mine[far, 1] = jnp.where(core == 0, part[half:], part[:half])
            crossing[far] = remote(
                mine.at[far, 1], crossed.at[far], cross_s.at[far], cross_r.at[far], partner
            )
            crossing[far].start()

    def deliver(far):
        crossing[far].wait_recv()
        both = mine[far, 0] + crossed[far]
        for index in range(per):
            tile, part = index // split, index % split
            piece = both[:, tile * LANES : (tile + 1) * LANES]
            rows = piece[part * block_rows : (part + 1) * block_rows]
            if rows.shape[0] < block_rows:
                rows = jnp.concatenate(
                    [rows, jnp.zeros((block_rows - rows.shape[0], LANES), F32)], axis=0
                )
            if far == 0:
                own32[index] = rows
            sbuf[far, index] = rows.astype(BF16)
        for near in range(1 if far == 0 else 0, per):
            sid = far * per + near
            sent[sid] = remote(
                sbuf.at[far, lax.rem(place + near, per)], inbox.at[sid], rs_s.at[sid],
                rs_r.at[sid], neighbour(sid),
            )
            sent[sid].start()

    order = (3, 2, 1, 0)
    produce(1)
    deliver(3)
    deliver(2)
    produce(0)
    deliver(1)
    deliver(0)

    lists = steps * KVH
    listed = chosen_ref[...] - base
    tile_of = listed >> 7
    lane_of = (listed & (LANES - 1)).astype(F32).T
    span_id = iota((8, spans), 1)
    out_row = jnp.zeros((8, spans), F32)
    for i in range(outl.shape[0]):
        out_row = jnp.where(span_id == outl[i] - base, 1.0, out_row)
    count = listed.shape[1]
    lane_id = iota((count, LANES), 1).astype(F32)
    tile_id = iota((8, count), 0)
    for i in range(lists):
        right = jnp.where(lane_of[:, i : i + 1] == lane_id, 1.0, 0.0).astype(BF16)
        left = jnp.where(tile_of[i : i + 1, :] == tile_id, 1.0, 0.0).astype(BF16)
        found = dot(left, right)
        for c in range(spans // LANES):
            here = slice(c * LANES, (c + 1) * LANES)
            live[i : i + 1, here] = jnp.maximum(found[c : c + 1], out_row[:1, here])
    rows_all = steps * QH
    at_row = iota((rows_all, lists), 0)
    wanted = at_row % steps * KVH + at_row // (steps * GROUP)
    widen = jnp.where(iota((rows_all, lists), 1) == wanted, 1.0, 0.0).astype(BF16)
    bias_out[...] = ((1.0 - dot(widen, live[...].astype(BF16))) * DEAD).astype(BF16)

    total = own32[place]
    for sid in range(1, chips):
        sent[sid].wait_recv()
        total = total + inbox[sid].astype(F32)
    full[core, chip] = total.astype(BF16)
    back = {}
    for sid in [far * per + near for far in order for near in range(per)]:
        if sid:
            back[sid] = remote(
                full.at[core, chip], full.at[core, chip], ag_s.at[sid], ag_r.at[sid],
                neighbour(sid),
            )
            back[sid].start()
    forward = {}
    forward[0] = remote(
        full.at[core, chip], full.at[core, chip], fwd_s.at[0], fwd_r.at[0], partner
    )
    forward[0].start()

    scale = 1.0 / (HD ** 0.5)
    cosq = cosq_ref[:steps, :]
    sinq = sinq_ref[:steps, :]

    def rope(x):
        return x * cosq + pltpu.roll(x, HALF, 1) * sinq

    for h in range(QH):
        x = q_ref[:, h * HD : (h + 1) * HD].astype(F32) * scale
        qrows[h * steps : (h + 1) * steps, :] = rope(x)
    list_rows = steps * GROUP
    lane = iota((list_rows, 8), 1)
    step_of = iota((list_rows, 8), 0) % steps
    reach = jnp.where(me == 0, 0, -steps)
    allowed = lane <= step_of + reach
    pad = jnp.zeros((8 - steps, HD), F32)
    zeros = jnp.zeros((list_rows, HD), F32)
    for g in range(KVH):
        columns = slice(g * HD, (g + 1) * HD)
        rows = slice(g * list_rows, (g + 1) * list_rows)
        q = qrows[rows, :]
        side = [q, zeros] if g % 2 == 0 else [zeros, q]
        at = g % 2 * list_rows
        qb_out[g // 2, at : at + list_rows, :] = jnp.concatenate(side, axis=1).astype(BF16)
        keys = rope(fk_ref[:, columns].astype(F32)).astype(BF16).astype(F32)
        keys = jnp.concatenate([keys, pad], axis=0)
        values = jnp.concatenate([fv_ref[:, columns].astype(F32), pad], axis=0)
        scores = jnp.where(allowed, dot(q, keys, NT, HIGHEST), DEAD)
        top = jnp.max(scores, axis=1, keepdims=True)
        weights = jnp.where(allowed, jnp.exp(scores - top), 0.0)
        init_out[0, rows, :] = dot(weights, values, NN, HIGHEST)
        init_out[1, rows, :] = jnp.broadcast_to(top, (list_rows, LANES))
        init_out[2, rows, :] = jnp.broadcast_to(
            jnp.sum(weights, axis=1, keepdims=True), (list_rows, LANES)
        )
    ang_copy.wait()
    for i in range(chunks):
        ang_out[i] = jnp.concatenate(
            [ang_land[:, i * 2 * TILES : (i + 1) * 2 * TILES]]
            + [jnp.zeros((HALF, LANES - 2 * TILES), F32)], axis=1
        )

    for sid in range(1, chips):
        source = source_chip(sid)
        remote(
            full.at[core, source], full.at[core, source], ag_s.at[sid], ag_r.at[sid],
            neighbour(sid),
        ).wait_recv()
        forward[sid] = remote(
            full.at[core, source], full.at[core, source], fwd_s.at[sid], fwd_r.at[sid], partner
        )
        forward[sid].start()
    for sid in range(chips):
        source = source_chip(sid)
        remote(
            full.at[other, source], full.at[other, source], fwd_s.at[sid], fwd_r.at[sid], partner
        ).wait_recv()
    for k in range(2):
        for q in range(chips):
            tile, part = q // split, q % split
            top = part * block_rows
            count = min(block_rows, half - top)
            sketch[k * half + top : k * half + top + count, tile * LANES : (tile + 1) * LANES] = (
                full[k, q, :count]
            )

    sk = sketch[...]
    gram = dot(sk, sk, NT)
    wide = m_ref.shape[1] // 2
    m_ref[...] = jnp.zeros_like(m_ref)
    m_ref[:, :rank] = gram
    m_ref[:, wide : wide + rank] = jnp.where(
        iota((rank, rank), 0) == iota((rank, rank), 1), 1.0, 0.0
    )
    eliminate(m_ref, rank)
    inverse = pieces(m_ref[:, wide : wide + rank], 3)
    basis = dot(inverse[0], sk) + dot(inverse[1], sk) + dot(inverse[2], sk)
    b_out[...] = basis.astype(BF16)
    bt_out[...] = basis.astype(BF16).T

    for far in range(regions):
        crossing[far].wait_send()
    for sid in range(chips):
        forward[sid].wait_send()
        if sid:
            sent[sid].wait_send()
            back[sid].wait_send()


def make_basis(s_t, cache_keys, queries, fresh_k, fresh_v, chosen, outliers, tables, devices):
    cosq, sinq, ang = tables
    rank, width = s_t.shape
    seq_len = cache_keys.shape[0]
    length = seq_len * devices
    steps = queries.shape[0]
    chips = devices // 2
    regions = width // (2 * LANES)
    per = chips // regions
    split = per // 2
    groups16 = rank // 2 // 16
    block_rows = 16 * (-(-groups16 // split))
    rows = steps * QH
    wide = -(-rank // LANES) * LANES
    spans = seq_len // SPAN
    dma = lambda *n: pltpu.SemaphoreType.DMA(n)
    anywhere = pl.BlockSpec(memory_space=pl.ANY)
    shape = jax.ShapeDtypeStruct
    block = (block_rows, LANES)
    return pl.pallas_call(
        functools.partial(basis_kernel, devices, length, steps),
        out_shape=(
            shape((rank, width), BF16),
            shape((width, rank), BF16),
            shape((PAIRS, rows // PAIRS, 2 * HD), BF16),
            shape((rows, spans), BF16),
            shape((3, rows, LANES), F32),
            shape((seq_len // CHUNK,) + ang.shape[1:], F32),
        ),
        in_specs=[
            pl.BlockSpec(memory_space=pltpu.SMEM), vmem(), anywhere, vmem(), vmem(), vmem(), vmem(),
            vmem(), vmem(), anywhere,
        ],
        out_specs=(vmem(),) * 6,
        scratch_shapes=[
            pltpu.VMEM(cache_keys.shape, BF16),
            pltpu.VMEM((rank, width), BF16),
            pltpu.VMEM((rank, seq_len), BF16),
            pltpu.VMEM((regions, 2, rank // 2, 2 * LANES), F32),
            pltpu.VMEM((regions, rank // 2, 2 * LANES), F32),
            pltpu.VMEM((regions, per) + block, BF16),
            pltpu.VMEM((per,) + block, F32),
            pltpu.VMEM((chips,) + block, BF16),
            pltpu.VMEM((2, chips) + block, BF16),
            pltpu.VMEM((rank, width), BF16),
            pltpu.VMEM((rank, 2 * wide), F32),
            pltpu.VMEM((rows, HD), F32),
            pltpu.VMEM((steps * KVH, spans), F32),
            pltpu.VMEM(ang.shape[1:], F32),
            dma(seq_len // CHUNK), dma(regions), dma(regions), dma(chips), dma(chips), dma(chips),
            dma(chips), dma(chips), dma(chips), pltpu.SemaphoreType.DMA,
        ],
        compiler_params=pltpu.CompilerParams(
            collective_id=0, has_side_effects=True, vmem_limit_bytes=VMEM_LIMIT
        ),
        name="key_basis",
    )(
        outliers, s_t, cache_keys, queries, fresh_k, fresh_v, chosen, cosq, sinq, ang,
    )


def attend_kernel(
    devices, outl, k_ref, v_ref, k_all, b_ref, bt_ref, qb_ref, bias_ref, init_ref, ang_ref,
    fine_ref, factor_ref, deal_ref, bx_ref, pos_ref, land, rhs, turn, keys, out, top, total, sems,
):
    step = pl.program_id(0)
    rank = b_ref.shape[0]
    rows = qb_ref.shape[1]
    half_rows = rows // 2

    @pl.when(step == 0)
    def _():
        spans = k_all.shape[0] // SPAN
        base = lax.axis_index("seq") * spans
        last = outl.shape[0] - 1
        before = jnp.int32(0)
        for i in range(outl.shape[0]):
            before = before + (outl[i] < base).astype(jnp.int32)
        place = iota((OMOST * SPAN, LANES), 0)
        target = jnp.full((OMOST * SPAN, LANES), -1, jnp.int32)
        copies = []
        for j in range(OMOST):
            index = before + j
            span = outl[jnp.minimum(index, last)] - base
            valid = (index <= last) & (span >= 0) & (span < spans)
            at = jnp.where(valid, span, 0)
            copy = pltpu.make_async_copy(
                k_all.at[pl.ds(pl.multiple_of(at * SPAN, SPAN), SPAN), :], land.at[j], sems.at[j]
            )
            copy.start()
            copies.append(copy)
            spot = jnp.where(valid, (at - j) * SPAN, -LANES * SPAN)
            target = jnp.where((place // SPAN == j) & (place + spot >= 0), place + spot, target)
        pos_ref[...] = target
        bx_ref[:, :rank] = bt_ref[...]
        out[...] = init_ref[0]
        top[...] = init_ref[1]
        total[...] = init_ref[2]
        token = iota((LANES, CHUNK), 1)
        spread = jnp.where(token // SPAN == iota((LANES, CHUNK), 0), 1.0, 0.0).astype(BF16)
        for p in range(PAIRS):
            keys[p, 2 * HD :, :] = spread
        for copy in copies:
            copy.wait()
        exact = jnp.concatenate([land[j].astype(F32) for j in range(OMOST)], axis=0)
        bx_ref[:, rank:] = exact.T.astype(BF16)

    cb, sb = fine_ref[0], fine_ref[1]
    ang = ang_ref[0]
    for i in range(TILES):
        here = slice(i * LANES, (i + 1) * LANES)
        ca, sa = ang[:, i : i + 1], ang[:, TILES + i : TILES + i + 1]
        turn[:HALF, here] = ca * cb - sa * sb
        turn[HALF:, here] = sa * cb + ca * sb

    factor = dot(b_ref[...], k_ref[...], NT)
    factor_ref[...] = factor
    lane = iota((pos_ref.shape[0], LANES), 1) + step * CHUNK
    for i in range(TILES):
        here = slice(i * LANES, (i + 1) * LANES)
        exact = jnp.where(pos_ref[...] == lane + i * LANES, 1.0, 0.0)
        rhs[rank:, here] = exact.astype(BF16)
        keep = 1.0 - jnp.sum(exact, axis=0, keepdims=True)
        rhs[:rank, here] = (factor[:, here] * keep).astype(BF16)

    def rebuild(first_head, heads, tokens):
        x = dot(bx_ref[first_head * HD : (first_head + heads) * HD, :], rhs[:, tokens])
        cosine, sine = turn[:HALF, tokens], turn[HALF:, tokens]
        for n in range(heads):
            head = first_head + n
            one, two = x[n * HD : n * HD + HALF], x[n * HD + HALF : (n + 1) * HD]
            p, at = head // 2, head % 2 * HD
            keys[p, at : at + HALF, tokens] = (one * cosine - two * sine).astype(BF16)
            keys[p, at + HALF : at + HD, tokens] = (two * cosine + one * sine).astype(BF16)

    def absorb(p, tokens):
        here = slice(p * rows, (p + 1) * rows)
        left = jnp.concatenate([qb_ref[p], bias_ref[here, :]], axis=1)
        scores = dot(left, keys[p, :, tokens])
        before = top[here, :]
        after = jnp.maximum(before, jnp.max(scores, axis=1, keepdims=True))
        weights = jnp.exp(scores - after[:, :1])
        scale = jnp.exp(before - after)
        top[here, :] = after
        total[here, :] = total[here, :] * scale + jnp.sum(weights, axis=1, keepdims=True)
        both = dot(weights.astype(BF16), v_ref[tokens, p * 2 * HD : (p + 1) * 2 * HD])
        own = jnp.concatenate([both[:half_rows, :HD], both[half_rows:, HD:]], axis=0)
        out[here, :] = out[here, :] * scale + own

    parts = [slice(t, t + 512) for t in range(0, CHUNK, 512)]
    for tokens in parts:
        for h in range(0, KVH, 8):
            rebuild(h, 8, tokens)
    for p in range(PAIRS):
        absorb(p, slice(0, CHUNK))

    @pl.when(step == pl.num_programs(0) - 1)
    def _():
        each = out.shape[0] // devices
        sums = total[...]
        mean = out[...] / jnp.where(sums > 0.0, sums, 1.0)
        level = jnp.where(sums > 0.0, top[...] + jnp.log(jnp.where(sums > 0.0, sums, 1.0)), DEAD)
        owner = iota((devices, out.shape[0]), 1) // each == iota((devices, out.shape[0]), 0)
        gather = jnp.where(owner, 1.0, 0.0).astype(BF16)
        spot = iota(level.shape, 0) % each == iota(level.shape, 1)
        level = [dot(gather, part) for part in pieces(jnp.where(spot, level, 0.0), 3)]
        rest = jnp.zeros((16 - each - 3, LANES), F32)
        for d in range(devices):
            here = slice(d * each, (d + 1) * each)
            deal_ref[d] = jnp.concatenate(
                [mean[here]] + [part[d : d + 1] for part in level] + [rest], axis=0
            ).astype(BF16)


def attend(cache_keys, cache_values, outliers, made, fine, devices):
    basis, bt, qb, bias, init, ang = made
    seq_len, width = cache_keys.shape
    rank = basis.shape[0]
    rows = init.shape[1]
    whole = lambda x: vmem(x.shape, lambda i: (0,) * len(x.shape))
    deal = (devices, 16, LANES)
    exact = OMOST * SPAN
    return pl.pallas_call(
        functools.partial(attend_kernel, devices),
        grid=(seq_len // CHUNK,),
        out_shape=(
            jax.ShapeDtypeStruct((rank, seq_len), F32),
            jax.ShapeDtypeStruct(deal, BF16),
        ),
        in_specs=[
            pl.BlockSpec(memory_space=pltpu.SMEM),
            vmem((CHUNK, width), lambda i: (i, 0)),
            vmem((CHUNK, width), lambda i: (i, 0)),
            pl.BlockSpec(memory_space=pl.ANY),
            whole(basis), whole(bt), whole(qb),
            vmem((rows, LANES), lambda i: (0, i)),
            whole(init),
            vmem((1,) + ang.shape[1:], lambda i: (i, 0, 0)),
            whole(fine),
        ],
        out_specs=(
            vmem((rank, CHUNK), lambda i: (0, i)),
            vmem(deal, lambda i: (0, 0, 0)),
        ),
        scratch_shapes=[
            pltpu.VMEM((width, rank + exact), BF16),
            pltpu.VMEM((exact, LANES), jnp.int32),
            pltpu.VMEM((OMOST, SPAN, width), BF16),
            pltpu.VMEM((rank + exact, CHUNK), BF16),
            pltpu.VMEM((HD, CHUNK), F32),
            pltpu.VMEM((PAIRS, 2 * HD + LANES, CHUNK), BF16),
            pltpu.VMEM((rows, LANES), F32),
            pltpu.VMEM((rows, LANES), F32),
            pltpu.VMEM((rows, LANES), F32),
            pltpu.SemaphoreType.DMA((OMOST,)),
        ],
        compiler_params=pltpu.CompilerParams(vmem_limit_bytes=VMEM_LIMIT),
        name="attend",
    )(outliers, cache_keys, cache_values, cache_keys, basis, bt, qb, bias, init, ang, fine)


def merge_kernel(devices, x_ref, out_ref, inbox, send_sem, recv_sem):
    me = lax.axis_index("seq")
    steps = out_ref.shape[0]
    heads = out_ref.shape[1] // HD
    rows = steps * heads

    def peer(off):
        return lax.rem(me + off, devices)

    barrier = pltpu.get_barrier_semaphore()
    for off in range(1, devices):
        pl.semaphore_signal(
            barrier, inc=1, device_id={"seq": peer(off)}, device_id_type=MESH
        )
    pl.semaphore_wait(barrier, devices - 1)
    copies = []
    for off in range(1, devices):
        copy = remote(
            x_ref.at[peer(off)], inbox.at[off], send_sem.at[off], recv_sem.at[off],
            {"seq": peer(off)},
        )
        copy.start()
        copies.append(copy)
    own = x_ref[me]
    spot = iota((rows, LANES), 1) == iota((rows, LANES), 0)

    def unpack(block):
        block = block.astype(F32)
        level = block[rows : rows + 1] + block[rows + 1 : rows + 2] + block[rows + 2 : rows + 3]
        level = jnp.sum(jnp.where(spot, level, 0.0), axis=1, keepdims=True)
        return block[:rows], level

    blocks = [unpack(own)]
    for off, copy in enumerate(copies):
        copy.wait_recv()
        blocks.append(unpack(inbox[off + 1]))
    joint = functools.reduce(jnp.maximum, [level for _, level in blocks])
    total = jnp.zeros((rows, 1), F32)
    summed = jnp.zeros((rows, HD), F32)
    for block, level in blocks:
        scale = jnp.exp(level - joint)
        total = total + scale
        summed = summed + block * scale
    result = summed / total
    for h in range(heads):
        out_ref[:, h * HD : (h + 1) * HD] = result[h * steps : (h + 1) * steps].astype(
            out_ref.dtype
        )
    for copy in copies:
        copy.wait_send()


def merge(x, steps):
    devices = x.shape[0]
    return pl.pallas_call(
        functools.partial(merge_kernel, devices),
        out_shape=jax.ShapeDtypeStruct((steps, QH // devices * HD), BF16),
        in_specs=[vmem()],
        out_specs=vmem(),
        scratch_shapes=[
            pltpu.VMEM(x.shape, BF16),
            pltpu.SemaphoreType.DMA((devices,)),
            pltpu.SemaphoreType.DMA((devices,)),
        ],
        compiler_params=pltpu.CompilerParams(collective_id=1, has_side_effects=True),
        name="merge",
    )(x)


def rotation_tables(seq_len, devices, steps):
    freq = np.exp(-np.log(THETA) * np.arange(HALF) * (2.0 / HD))
    fine = np.arange(LANES)[None, :] * freq[:, None]
    fine = np.stack([np.cos(fine), np.sin(fine)]).astype(np.float32)
    coarse = np.arange(seq_len * devices // LANES).reshape(devices, -1, 1, TILES) * LANES
    coarse = coarse * freq[:, None]
    coarse = np.concatenate([np.cos(coarse), np.sin(coarse)], axis=3)
    ang = np.zeros((devices, HALF, LANES), np.float32)
    ang[:, :, : coarse.shape[1] * 2 * TILES] = np.moveaxis(coarse, 1, 2).reshape(
        devices, HALF, -1
    )
    decoded = (seq_len * devices + np.arange(8))[:, None] * freq
    cosq = np.concatenate([np.cos(decoded)] * 2, axis=1).astype(np.float32)
    sinq = np.concatenate([-np.sin(decoded), np.sin(decoded)], axis=1).astype(np.float32)
    return fine, ang, cosq, sinq


def on_device(
    cache_keys,
    cache_values,
    sketch_matrix,
    queries,
    fresh_keys,
    fresh_values,
    chosen,
    shard_counts,
    outliers,
):
    devices = lax.axis_size("seq")
    steps = queries.shape[0]
    fine, ang, cosq, sinq = rotation_tables(cache_keys.shape[0], devices, steps)
    made = make_basis(
        sketch_matrix.T, cache_keys, queries, fresh_keys, fresh_values,
        chosen.reshape(steps * KVH, chosen.shape[2]), outliers, (cosq, sinq, ang), devices,
    )
    factor_t, parts = attend(cache_keys, cache_values, outliers, made, fine, devices)
    return (merge(parts, steps), factor_t.T)


def solution(mesh):
    in_specs = (
        P(("groups", "seq"), None),
        P(("groups", "seq"), None),
        P(),
        P("groups", None),
        P("groups", None),
        P("groups", None),
        P("groups", None, None),
        P("groups", None, None),
        P("groups"),
    )
    out_specs = (P("groups", "seq"), P(("groups", "seq"), None))
    return jax.shard_map(
        on_device, mesh=mesh, in_specs=in_specs, out_specs=out_specs, check_vma=False
    )
```
